32 devices in a mesh: grp: 4 (over y, core), row: 8 (over z, x).
Axes of the slice: x: 2, y: 2, z: 4, core: 2. Of those that a mesh axis runs over, the one named last changes fastest.
Arguments:
- labeled: bfloat16 [4, 1024, 1024], P(None, 'row', 'grp'), may hold values from -6 to 6
- candidates: bfloat16 [4096, 1024], P(('grp', 'row')), may hold values from -6 to 6
- factor_rows: bfloat16 [4, 1024, 4096], P(None, 'row'), may hold values from -6 to 6
- block_inverse: bfloat16 [4, 1024, 1024], P(None, 'row'), as said below
Outputs:
- whitened: bfloat16 [4, 1024, 4096], P(None, 'row', 'grp')
- explained: float32 [4096], P('grp')
The draws below stay inside these ranges and needn't reach their ends.
Inputs may be any that keep to these rules, and one draw needn't show every extreme that they name: Each block of block_inverse is lower triangular with a positive diagonal; it is given as is and is not derived from factor_rows.
All inputs are finite; a program needn't handle non-finite values.
Results may differ from the reference program's by a relative error of at most 0.0075.
Values may be sent and summed in bfloat16 or wider, within the bound.
No kernel may reach another device: no remote copies, remote signals or barrier semaphores. Data moves between devices by JAX's collectives and lax.ppermute only.
A program may use at most 64 MiB of HBM per device.

```python
import math
import jax
import jax.numpy as jnp
from jax import lax

F = 1024
B = 1024
NB = 4
NC = 4096
N = 4096


def draw_block_inverse(key, part):
    key_scale = jax.random.fold_in(key, 11)
    key_noise = jax.random.fold_in(key, 12)
    position = jnp.arange(B).astype(jnp.float32)
    base = jnp.exp(jax.random.uniform(key_scale, (NB, B), jnp.float32, math.log(1.0 / 150.0), math.log(1.0 / 60.0)))
    base = base * jnp.exp(math.log(3.0) * position / B)[None, :]
    noise = jax.random.normal(key_noise, (NB, B, B), jnp.float32)
    lower = (position[:, None] > position[None, :]).astype(jnp.float32)
    diagonal = (position[:, None] == position[None, :]).astype(jnp.float32)
    spread = 0.3 / jnp.sqrt(position + 1.0)
    entries = noise * lower[None] * (base * spread[None, :])[:, :, None] + diagonal[None] * base[:, :, None]
    return entries.astype(jnp.bfloat16)


def block_levels(stream_key, shape, cuts, low, top_value):
    factor_of = 1.0
    for axis_at, blocks in cuts:
        steps = jax.random.uniform(jax.random.fold_in(jax.random.fold_in(stream_key, 6), axis_at), (blocks,), jnp.float32, low / len(cuts), top_value / len(cuts))
        factor_of = factor_of * jnp.repeat(jnp.exp(steps), shape[axis_at] // blocks).reshape((-1,) + (1,) * (len(shape) - 1 - axis_at))
    return factor_of


def bell_draw(stream_key, extent, scale, limit, pieces=(), kind=jnp.bfloat16):
    loudness = block_levels(stream_key, extent, pieces, -0.22, 0.18) if pieces else 1.0
    drawn = jax.random.normal(stream_key, extent, jnp.float32) * scale * loudness
    return jnp.minimum(jnp.maximum(drawn, -limit), limit).astype(kind)


def setup_inputs(seed: int = 0) -> dict:
    splits = jax.random.split(jax.random.key(seed), 5)
    return {
        "labeled": bell_draw(splits[0], (NB, B, F), 1.0, 6.0, ((1, 8), (2, 4))),
        "candidates": bell_draw(splits[1], (NC, F), 1.0, 6.0, ((0, 32),)),
        "factor_rows": bell_draw(splits[2], (NB, B, N), 1.0, 6.0, ((1, 8),)),
        "block_inverse": draw_block_inverse(jax.random.fold_in(splits[4], 71), 0),
    }


def reference(labeled, candidates, factor_rows, block_inverse):
    kernel_scale = 0.5 / math.sqrt(F)
    flat_rows = labeled.reshape(NB * B, F)
    kernel = jnp.exp(jnp.dot(flat_rows, candidates.T, preferred_element_type=jnp.float32) * kernel_scale)
    solved = []
    for number in range(NB):
        residual = kernel[number * B:(number + 1) * B]
        if number > 0:
            earlier = jnp.concatenate(solved, axis=0)
            residual = residual - jnp.dot(factor_rows[number][:, :number * B], earlier, preferred_element_type=jnp.float32)
        residual = residual.astype(jnp.bfloat16)
        solved.append(jnp.dot(block_inverse[number], residual, preferred_element_type=jnp.float32).astype(jnp.bfloat16))
    whitened = jnp.stack(solved, axis=0)
    explained = lax.optimization_barrier(jnp.sum(jnp.square(whitened.astype(jnp.float32)), axis=(0, 1)))
    return (whitened, explained)
```

```python
import math

import jax
import jax.numpy as jnp
from jax import lax
from jax.experimental import pallas as pl
from jax.experimental.pallas import tpu as pltpu
from jax.sharding import PartitionSpec as P

BF = jnp.bfloat16
F32 = jnp.float32


def gathered_on_device(labeled, candidates, factor_rows, block_inverse):
    gathered = lax.all_gather(labeled, "grp", axis=2, tiled=True)
    block_count, own_count, feature_width = gathered.shape
    block_size = block_inverse.shape[2]
    kernel_scale = 0.5 / math.sqrt(feature_width)
    flat_rows = gathered.reshape(block_count * own_count, feature_width)
    kernel = jnp.exp(
        jnp.dot(
            flat_rows,
            lax.all_gather(candidates, "row", axis=0, tiled=True).T,
            preferred_element_type=F32,
        )
        * kernel_scale
    )
    cand_count = kernel.shape[1]
    kernel = kernel.reshape(block_count, own_count, cand_count)
    pending = [kernel[number] for number in range(block_count)]
    solved_own = []
    for number in range(block_count):
        rounded = pending[number].astype(BF)
        residual_block = lax.all_gather(rounded, "row", axis=0, tiled=True)
        own_rows = jnp.dot(
            block_inverse[number], residual_block, preferred_element_type=F32
        ).astype(BF)
        solved_own.append(own_rows)
        if number + 1 < block_count:
            solved = lax.all_gather(own_rows, "row", axis=0, tiled=True)
            panel = factor_rows[
                number + 1 :, :, number * block_size : (number + 1) * block_size
            ]
            later_count = block_count - number - 1
            updates = jnp.dot(
                panel.reshape(later_count * own_count, block_size),
                solved,
                preferred_element_type=F32,
            ).reshape(later_count, own_count, cand_count)
            for later in range(later_count):
                at = number + 1 + later
                pending[at] = pending[at] - updates[later]
    whitened = jnp.stack(solved_own, axis=0)
    squares = jnp.sum(jnp.square(whitened.astype(F32)), axis=(0, 1))
    return (whitened, lax.psum(squares, "row"))


def swap(x, axis, size, bit):
    return lax.ppermute(x, axis, [(i, i ^ bit) for i in range(size)])


def ring_order(n):
    return [2 * p if p < n // 2 else 2 * (n - 1 - p) + 1 for p in range(n)]


def ring_gather(x, n):
    order = ring_order(n)
    up = [(order[p], order[(p + 1) % n]) for p in range(n)]
    down = [(b, a) for a, b in up]
    ahead, behind = [x], [x]
    for _ in range(n // 2 - 1):
        ahead.append(lax.ppermute(ahead[-1], "row", up))
        behind.append(lax.ppermute(behind[-1], "row", down))
    half = x.shape[0] // 2
    far_a = lax.ppermute(ahead[-1][:half], "row", up)
    far_b = lax.ppermute(behind[-1][half:], "row", down)
    far = jnp.concatenate([far_a, far_b], axis=0)
    return ahead + [far] + behind[1:]


def ring_sources(r, n):
    pos = jnp.where(r % 2 == 0, r // 2, n - 1 - r // 2)
    away = jnp.array(
        [-k for k in range(n // 2 + 1)] + [k for k in range(1, n // 2)], jnp.int32
    )
    p = (pos + away + n) % n
    return jnp.where(p < n // 2, 2 * p, 2 * (n - 1 - p) + 1).astype(jnp.int32)


def call(body, outs, args, flops, scratch=()):
    vm = pl.BlockSpec(memory_space=pltpu.VMEM)
    sm = pl.BlockSpec(memory_space=pltpu.SMEM)
    moved = sum(a.size * a.dtype.itemsize for a in args)
    moved += sum(math.prod(o.shape) * o.dtype.itemsize for o in outs)
    return pl.pallas_call(
        body,
        out_shape=outs,
        in_specs=[sm] + [vm] * (len(args) - 1),
        out_specs=[vm] * len(outs),
        scratch_shapes=list(scratch),
        compiler_params=pltpu.CompilerParams(vmem_limit_bytes=24 * 1024 * 1024),
        cost_estimate=pl.CostEstimate(
            flops=flops, bytes_accessed=moved, transcendentals=0
        ),
    )(*args)


def sds(*shape, dtype=BF):
    return jax.ShapeDtypeStruct(shape, dtype)


def split_on_device(G, R, labeled, candidates, factor_rows, block_inverse):
    nb, own, fw = labeled.shape
    cown, feat = candidates.shape
    bs = block_inverse.shape[2]
    q = own // G
    cw = G * cown
    scale = 0.5 / math.sqrt(feat)
    g = lax.axis_index("grp")
    r = lax.axis_index("row")
    y, c = g // 2, g % 2
    where_idx = jnp.concatenate(
        [jnp.stack([g, g ^ 2, g ^ 1, g ^ 3, y, c, r, r]).astype(jnp.int32), ring_sources(r, R)]
    )

    cand_y = swap(candidates, "grp", G, 2)
    cand_c = swap(candidates, "grp", G, 1)
    cand_yc = swap(cand_y, "grp", G, 1)

    hq = own // 2
    keep = lax.dynamic_slice_in_dim(labeled, y * hq, hq, 1)
    sent = lax.dynamic_slice_in_dim(labeled, (1 - y) * hq, hq, 1)
    got = swap(sent, "grp", G, 2)
    low = jnp.where(y == 0, keep, got)
    high = jnp.where(y == 0, got, keep)
    pair = jnp.concatenate([low, high], axis=2)
    keep = lax.dynamic_slice_in_dim(pair, c * q, q, 1)
    sent = lax.dynamic_slice_in_dim(pair, (1 - c) * q, q, 1)
    got = swap(sent, "grp", G, 1)
    even = jnp.where(c == 0, keep, got)
    odd = jnp.where(c == 0, got, keep)
    lab_q = jnp.concatenate(
        [even[..., :fw], odd[..., :fw], even[..., fw:], odd[..., fw:]], axis=2
    )

    inv_q = lax.dynamic_slice_in_dim(block_inverse, g * q, q, 1)
    slabs = []
    for b in range(nb):
        parts = [lab_q[b], inv_q[b]]
        if b:
            panel = lax.dynamic_slice(factor_rows, (b, g * q, 0), (1, q, b * bs))[0]
            parts += [panel[:, j * bs : (j + 1) * bs] for j in range(b)]
        slabs.append(ring_gather(jnp.concatenate(parts, axis=0), R))

    def rows_of(refs, part):
        return jnp.concatenate([s[part * q : (part + 1) * q, :] for s in refs], axis=0)

    def nt(a, b):
        return lax.dot_general(
            a, b, (((1,), (1,)), ((), ())), preferred_element_type=F32
        )

    qr = R * q
    half_rows = bs // 2

    def k0_body(idx, ca, cb, cc, cd, *rest):
        refs, (res, cn) = rest[:R], rest[R:]
        for slot, ref in enumerate((ca, cb, cc, cd)):
            cn[pl.ds(pl.multiple_of(idx[slot] * cown, cown), cown), :] = ref[...]
        s = nt(rows_of(refs, 0), cn[...])
        k = jnp.exp(s * scale).astype(BF)
        for t in range(R):
            at = pl.multiple_of(idx[8 + t] * q, q)
            res[pl.ds(at, q), :] = k[t * q : (t + 1) * q, :]

    res, cn = call(
        k0_body,
        [sds(qr, cw), sds(cw, feat)],
        [where_idx, candidates, cand_y, cand_c, cand_yc] + slabs[0],
        2 * qr * cw * feat,
    )

    def k_body(idx, cref, *rest):
        refs, (out,) = rest[:R], rest[R:]
        out[...] = jnp.exp(nt(rows_of(refs, 0), cref[...]) * scale)

    kernels = [None] + [
        call(
            k_body,
            [sds(qr, cw, dtype=F32)],
            [where_idx, cn] + slabs[b],
            2 * qr * cw * feat,
        )[0]
        for b in range(1, nb)
    ]

    def solve_body(idx, a, b, cc, d, iq, iy, out, full):
        width = a.shape[1]
        for slot, ref in enumerate((a, b, cc, d)):
            gq = pl.multiple_of(idx[slot] * q, q)
            for t in range(R):
                full[pl.ds(t * own + gq, q), :] = ref[t * q : (t + 1) * q, :]
        for side, ref in enumerate((iq, iy)):
            o = jnp.dot(ref[...], full[...], preferred_element_type=F32).astype(BF)
            yy = idx[4] if side == 0 else 1 - idx[4]
            for t in range(R):
                at = pl.multiple_of(idx[8 + t] * (2 * q) + yy * q, q)
                out[pl.ds(at, q), :] = o[t * q : (t + 1) * q, :]

    def solve(b, pieces):
        iq = jnp.concatenate([s[q : 2 * q, :] for s in slabs[b]], axis=0)
        iy = swap(iq, "grp", G, 2)
        width = pieces[0].shape[1]
        return call(
            solve_body,
            [sds(half_rows, width)],
            [where_idx] + pieces + [iq, iy],
            2 * half_rows * bs * width,
            [pltpu.VMEM((bs, width), BF)],
        )[0]

    def place_halves(idx, mine, theirs, put):
        for side, ref in enumerate((mine, theirs)):
            cc = idx[5] if side == 0 else 1 - idx[5]
            for t in range(R):
                for yy in range(2):
                    at = pl.multiple_of(t * own + yy * 2 * q + cc * q, q)
                    put(t, yy, cc, at, ref, (t * 2 + yy) * q)

    solved = []
    for b in range(nb - 1):
        other_y = swap(res, "grp", G, 2)
        other_c = swap(res, "grp", G, 1)
        other_yc = swap(other_y, "grp", G, 1)
        mine = solve(b, [res, other_y, other_c, other_yc])
        theirs = swap(mine, "grp", G, 1)
        last = b + 1 == nb - 1

        def update_body(idx, mine_ref, theirs_ref, kref, *rest, b=b, last=last):
            prev, rest = rest[:b], rest[b:]
            refs, rest = rest[:R], rest[R:]
            wfull, out = rest[0], rest[1]

            def put(t, yy, cc, at, ref, src):
                wfull[pl.ds(at, q), :] = ref[src : src + q, :]

            place_halves(idx, mine_ref, theirs_ref, put)
            acc = kref[...]
            for j in range(b + 1):
                w = wfull if j == b else prev[j]
                acc = acc - jnp.dot(
                    rows_of(refs, 2 + j), w[...], preferred_element_type=F32
                )
            v = acc.astype(BF)
            if last:
                lo, hi = v[:, : cw // 2], v[:, cw // 2 :]
                first = idx[4] == 0
                keep_v = jnp.where(first, lo, hi)
                send_v = jnp.where(first, hi, lo)
            for t in range(R):
                at = pl.multiple_of(idx[8 + t] * q, q)
                cut = slice(t * q, (t + 1) * q)
                if last:
                    out[pl.ds(at, q), :] = keep_v[cut, :]
                    rest[2][pl.ds(at, q), :] = send_v[cut, :]
                else:
                    out[pl.ds(at, q), :] = v[cut, :]

        outs = [sds(bs, cw)]
        outs += [sds(qr, cw // 2)] * 2 if last else [sds(qr, cw)]
        got = call(
            update_body,
            outs,
            [where_idx, mine, theirs, kernels[b + 1]] + solved + slabs[b + 1],
            2 * qr * bs * (b + 1) * cw,
        )
        solved.append(got[0])
        res = got[1:]
        if not last:
            res = res[0]

    keep_v, send_v = res
    other_y = swap(send_v, "grp", G, 2)
    other_c = swap(keep_v, "grp", G, 1)
    other_yc = swap(other_y, "grp", G, 1)
    mine = solve(nb - 1, [keep_v, other_y, other_c, other_yc])
    mine_l, mine_r = mine[:, :cown], mine[:, cown:]
    keep_w = jnp.where(c == 0, mine_l, mine_r)
    send_w = jnp.where(c == 0, mine_r, mine_l)
    theirs = swap(send_w, "grp", G, 1)

    extra = 16

    def pack_body(idx, mine_ref, theirs_ref, *rest):
        prev, (out,) = rest[: nb - 1], rest[nb - 1 :]
        lane = pl.multiple_of(idx[0] * cown, cown)
        total = jnp.zeros((1, cown), F32)
        for b in range(nb - 1):
            for t in range(R):
                v = prev[b][t * own : (t + 1) * own, pl.ds(lane, cown)]
                out[t, b * own : (b + 1) * own, :] = v
                v = v.astype(F32)
                total = total + jnp.sum(v * v, axis=0, keepdims=True)
        for side, ref in enumerate((mine_ref, theirs_ref)):
            cc = idx[5] if side == 0 else 1 - idx[5]
            v = ref[...].astype(F32)
            total = total + jnp.sum(v * v, axis=0, keepdims=True)
            for t in range(R):
                for yy in range(2):
                    at = pl.multiple_of((nb - 1) * own + yy * 2 * q + cc * q, q)
                    src = (t * 2 + yy) * q
                    out[t, pl.ds(at, q), :] = ref[src : src + q, :]
        head = total.astype(BF).astype(F32)
        tail = total - head
        row = lax.broadcasted_iota(jnp.int32, (extra, cown), 0)
        block = jnp.where(row == 0, head, jnp.where(row == 1, tail, 0.0)).astype(BF)
        for t in range(R):
            out[t, nb * own :, :] = block

    packed = call(
        pack_body,
        [sds(R, nb * own + extra, cown)],
        [where_idx, keep_w, theirs] + solved,
        4 * bs * nb * cown,
    )[0]
    landed = lax.all_to_all(packed, "row", split_axis=0, concat_axis=0, tiled=True)

    def unpack_body(idx, ref, out, sums):
        for t in range(R):
            for b in range(nb):
                out[b, :, t * cown : (t + 1) * cown] = ref[t, b * own : (b + 1) * own, :]
            tail = ref[t, nb * own :, :].astype(F32)
            sums[t : t + 1, :] = tail[0:1, :] + tail[1:2, :]

    whitened, sums = call(
        unpack_body,
        [sds(nb, own, R * cown), sds(R, cown, dtype=F32)],
        [where_idx, landed],
        R * cown,
    )
    return (whitened, sums.reshape(R * cown))


def solution(mesh):
    G, R = mesh.shape["grp"], mesh.shape["row"]

    def on_device(labeled, candidates, factor_rows, block_inverse):
        own = labeled.shape[1]
        fits = G == 4 and R % 2 == 0 and own % (16 * G) == 0
        fits = fits and candidates.shape[0] % 128 == 0
        if fits:
            return split_on_device(
                G, R, labeled, candidates, factor_rows, block_inverse
            )
        return gathered_on_device(labeled, candidates, factor_rows, block_inverse)

    in_specs = (
        P(None, "row", "grp"),
        P(("grp", "row"), None),
        P(None, "row", None),
        P(None, "row", None),
    )
    out_specs = (P(None, "row", "grp"), P("grp"))
    return jax.shard_map(
        on_device, mesh=mesh, in_specs=in_specs, out_specs=out_specs, check_vma=False
    )
```
